256 devices in a mesh: section: 8 (over y, core), dp: 32 (over x, z).
Axes of the slice: x: 4, y: 4, z: 8, core: 2. Of those that a mesh axis runs over, the one named last changes fastest.
Arguments:
- inputs: bfloat16 [6144, 4096], P('dp'), may hold values from -6 to 6
- output_cotangent: bfloat16 [6144, 4096], P('dp'), may hold values from -6 to 6
- lengths: int32 [64], P('dp'), may hold values from 24 to 96
- query_examples: int32 [16], replicated, may hold values from 0 to 63
- norm_gain: bfloat16 [8, 4096], P('section'), may hold values from 0.5 to 1.5
- value_weight: bfloat16 [8, 4096, 1024], P('section', 'dp'), may hold values from -0.09375 to 0.09375
- output_weight: bfloat16 [8, 4096, 1024], P('section', 'dp'), may hold values from -0.1875 to 0.1875
- input_projection: bfloat16 [8, 32, 4096], P('section'), may hold values from -0.09375 to 0.09375
- output_projection: bfloat16 [8, 32, 1024], P('section'), may hold values from -0.1875 to 0.1875
- fisher_prior: float32 [8, 1024, 1024], P('section'), as said below
Outputs:
- scores: float32 [64, 16], P('dp')
The draws below stay inside these ranges and needn't reach their ends.
Inputs may be any that keep to these rules, and one draw needn't show every extreme that they name: `fisher_prior`: each block's 1024 x 1024 matrix is symmetric and positive definite.
All inputs are finite; a program needn't handle non-finite values.
Results may differ from the reference program's by a relative error of at most 0.0013.
Values may be sent and summed in bfloat16 or wider, within the bound.
No kernel may reach another device: no remote copies, remote signals or barrier semaphores. Data moves between devices by JAX's collectives and lax.ppermute only.
A program may use at most 128 MiB of HBM per device.

```python
import math
import jax
import jax.numpy as jnp
from jax import lax

D = 4096
KV = 1024
RI = 32
RO = 32
LEN = 96
QUERIES = 16
SECTIONS = 8
EXAMPLES = 64
TOKENS = 6144
K = 1024


def draw_fisher_prior(key, part):
    factor_key, diagonal_key = jax.random.split(key, 2)
    factors = jax.random.normal(factor_key, (SECTIONS, K, K), jnp.float32)
    shared = jnp.einsum('sij,skj->sik', factors, factors, precision=lax.Precision.HIGHEST) / K
    spread = jnp.exp(jax.random.uniform(diagonal_key, (SECTIONS, K), jnp.float32, math.log(0.5), math.log(4.0)))
    prior_matrix = shared + spread[:, :, None] * jnp.eye(K, dtype=jnp.float32)[None]
    return prior_matrix


def plant(entries, rng, low, high):
    index_at = [jax.random.randint(jax.random.fold_in(rng, axis), (), 0, length) for axis, length in enumerate(entries.shape)]
    longest = entries.shape.index(max(entries.shape))
    beside = index_at[:longest] + [(index_at[longest] + 1) % entries.shape[longest]] + index_at[longest + 1:]
    return entries.at[tuple(index_at)].set(low).at[tuple(beside)].set(high)


def shard_levels(stream_key, shape, cuts, least, largest):
    level, own = 1.0, jax.random.fold_in(stream_key, 6)
    for axis_at, shards_of in cuts:
        draws = jnp.exp(jax.random.uniform(jax.random.fold_in(own, axis_at), (shards_of,), jnp.float32, least / len(cuts), largest / len(cuts)))
        level = level * jnp.repeat(draws, shape[axis_at] // shards_of).reshape([-1 if axis == axis_at else 1 for axis in range(len(shape))])
    return level


def centred(rng, shape, width, most, pieces=(), kind=jnp.bfloat16):
    entries = jax.random.normal(rng, shape, jnp.float32) * width
    if len(pieces) > 0:
        entries = shard_levels(rng, shape, pieces, -0.22, 0.18) * entries
    return jnp.clip(entries, min=-most, max=most).astype(kind)


def setup_inputs(seed: int = 0) -> dict:
    splits = jax.random.split(jax.random.key(seed), 11)
    inputs = centred(splits[0], (TOKENS, D), 1.0, 6.0, ((0, 32),))
    output_cotangent = centred(splits[1], (TOKENS, D), 1.0, 6.0, ((0, 32),))
    lengths = plant(jax.random.randint(splits[2], (EXAMPLES,), LEN // 4, LEN + 1), jax.random.fold_in(splits[2], 1), LEN // 4, LEN).astype(jnp.int32)
    query_examples = plant(jax.random.randint(splits[3], (QUERIES,), 0, EXAMPLES), jax.random.fold_in(splits[3], 1), 0, EXAMPLES - 1).astype(jnp.int32)
    norm_gain = jnp.clip(1.0 + 0.1 * jax.random.normal(splits[4], (SECTIONS, D), jnp.float32), 0.5, 1.5).astype(jnp.bfloat16)
    value_weight = centred(splits[5], (SECTIONS, D, KV), D ** -0.5, 0.09375, ((0, 8), (1, 32)))
    output_weight = centred(splits[6], (SECTIONS, D, KV), KV ** -0.5, 0.1875, ((0, 8), (1, 32)))
    input_projection = centred(splits[7], (SECTIONS, RI, D), D ** -0.5, 0.09375, ((0, 8),))
    output_projection = centred(splits[8], (SECTIONS, RO, KV), KV ** -0.5, 0.1875, ((0, 8),))
    fisher_prior = draw_fisher_prior(jax.random.fold_in(splits[10], 71), 0)
    return dict(inputs=inputs, output_cotangent=output_cotangent, lengths=lengths, query_examples=query_examples, norm_gain=norm_gain, value_weight=value_weight, output_weight=output_weight, input_projection=input_projection, output_projection=output_projection, fisher_prior=fisher_prior)


def normalize(hidden, gain):
    widened = hidden.astype(jnp.float32)
    factor = lax.rsqrt(lax.optimization_barrier(jnp.mean(widened * widened, axis=-1, keepdims=True)) + 1e-05)
    return (widened * factor * gain.astype(jnp.float32)).astype(jnp.bfloat16)

def forward_block(hidden, gain, value_map, output_map, input_map):
    normed = normalize(hidden, gain)
    values = jnp.dot(normed.astype(jnp.float32), value_map.astype(jnp.float32), preferred_element_type=jnp.float32)
    activated = jax.nn.silu(values).astype(jnp.bfloat16)
    branch = lax.dot_general(activated.astype(jnp.float32), output_map.astype(jnp.float32), (((1,), (1,)), ((), ())), preferred_element_type=jnp.float32)
    following = (hidden.astype(jnp.float32) + branch).astype(jnp.bfloat16)
    features = lax.dot_general(normed.astype(jnp.float32), input_map.astype(jnp.float32), (((1,), (1,)), ((), ())), preferred_element_type=jnp.float32).astype(jnp.bfloat16)
    return (following, values, features)

def backward_block(hidden, values, cotangent, gain, value_map, output_map, output_map_small):
    widened = hidden.astype(jnp.float32)
    factor = lax.rsqrt(lax.optimization_barrier(jnp.mean(widened * widened, axis=-1, keepdims=True)) + 1e-05)
    upstream = jnp.dot(cotangent.astype(jnp.float32), output_map.astype(jnp.float32), preferred_element_type=jnp.float32)
    logistic = jax.nn.sigmoid(values)
    slopes = (upstream * logistic * (1.0 + values * (1.0 - logistic))).astype(jnp.bfloat16)
    signals = lax.dot_general(slopes.astype(jnp.float32), output_map_small.astype(jnp.float32), (((1,), (1,)), ((), ())), preferred_element_type=jnp.float32).astype(jnp.bfloat16)
    normed_grad = lax.dot_general(slopes.astype(jnp.float32), value_map.astype(jnp.float32), (((1,), (1,)), ((), ())), preferred_element_type=jnp.float32)
    weighted = normed_grad * gain.astype(jnp.float32)
    inner_mean = lax.optimization_barrier(jnp.mean(weighted * widened, axis=-1, keepdims=True))
    hidden_grad = factor * weighted - widened * (factor * factor * factor) * inner_mean
    previous = (cotangent.astype(jnp.float32) + hidden_grad).astype(jnp.bfloat16)
    return (previous, signals)

def reference(inputs, output_cotangent, lengths, query_examples, norm_gain, value_weight, output_weight, input_projection, output_projection, fisher_prior):
    positions = jnp.arange(LEN, dtype=jnp.int32)
    keep = (positions[None, :] < lengths[:, None]).astype(jnp.bfloat16)
    hidden = inputs
    stored_hidden = []
    stored_values = []
    stored_features = []
    for section in range(SECTIONS):
        stored_hidden.append(hidden)
        hidden, values, features = forward_block(hidden, norm_gain[section], value_weight[section], output_weight[section], input_projection[section])
        stored_values.append(values)
        stored_features.append(features)
    cotangent = (output_cotangent.reshape(EXAMPLES, LEN, D) * keep[:, :, None]).reshape(TOKENS, D)
    scores = jnp.zeros((EXAMPLES, QUERIES), jnp.float32)
    for section in reversed(range(SECTIONS)):
        cotangent, signals = backward_block(stored_hidden[section], stored_values[section], cotangent, norm_gain[section], value_weight[section], output_weight[section], output_projection[section])
        grads = jnp.einsum('elo,eli->eoi', signals.reshape(EXAMPLES, LEN, RO).astype(jnp.float32), stored_features[section].reshape(EXAMPLES, LEN, RI).astype(jnp.float32), precision=lax.Precision.HIGHEST) / LEN
        flat = grads.reshape(EXAMPLES, K)
        fisher = jnp.dot(flat.T, flat, precision=lax.Precision.HIGHEST)
        hessian = fisher_prior[section] + fisher
        chosen = flat[query_examples]
        lower_factor = jnp.linalg.cholesky(hessian)
        solved = jax.scipy.linalg.cho_solve((lower_factor, True), chosen.T)
        scores = scores + jnp.dot(flat, solved, precision=lax.Precision.HIGHEST)
    return scores
```

```python
import jax
import jax.numpy as jnp
from jax import lax
from jax.experimental import pallas as pl
from jax.experimental.pallas import tpu as pltpu
from jax.sharding import PartitionSpec as P

EXACT = lax.Precision.HIGHEST
BLOCK = 128
CHUNK = 512
f32 = jnp.float32
bf16 = jnp.bfloat16
NT = (((1,), (1,)), ((), ()))
TN = (((0,), (0,)), ((), ()))
MEBI = 1 << 20


def whole():
    return pl.BlockSpec(memory_space=pltpu.VMEM)


def swept(block):
    size = block.shape[0]
    lanes = lax.broadcasted_iota(jnp.int32, (1, size), 1)
    rows = lax.broadcasted_iota(jnp.int32, (size, 1), 0)
    for at in range(size):
        column = block[:, at : at + 1]
        row = block[at : at + 1, :]
        inverse = 1.0 / column[at : at + 1, :]
        scaled = jnp.where(lanes == at, -inverse, row * inverse)
        column = jnp.where(rows == at, -1.0, column)
        kept = jnp.where((lanes == at) | (rows == at), 0.0, block)
        block = kept - column * scaled
    return block


def exact_dot(a, b):
    return jnp.dot(a, b, precision=EXACT, preferred_element_type=f32)


def inverse_kernel(prior, out):
    size = prior.shape[0]
    tall = min(256, size)
    out[...] = prior[...]

    def step(turn, _):
        span = pl.ds(pl.multiple_of(turn * BLOCK, BLOCK), BLOCK)
        pivot = swept(out[span, span])
        left = out[:, span]
        above = out[span, :]
        right = -exact_dot(left, pivot)
        below = -exact_dot(pivot, above)
        for row in range(0, size, tall):
            out[row : row + tall, :] -= exact_dot(right[row : row + tall], above)
        out[:, span] = right
        out[span, :] = below
        out[span, span] = pivot
        return 0

    lax.fori_loop(0, size // BLOCK, step, 0)


def minus_inverse(prior):
    size = prior.shape[0]
    return pl.pallas_call(
        inverse_kernel,
        out_shape=jax.ShapeDtypeStruct(prior.shape, f32),
        in_specs=[whole()],
        out_specs=whole(),
        compiler_params=pltpu.CompilerParams(vmem_limit_bytes=32 * MEBI),
        cost_estimate=pl.CostEstimate(
            flops=60 * size**3, bytes_accessed=8 * size * size, transcendentals=0
        ),
        name="prior_inverse",
    )(prior)


def inverse_root(hidden):
    return lax.rsqrt(jnp.mean(hidden * hidden, axis=-1, keepdims=True) + 1e-05)


def forward_kernel(
    flags, entry, incoming, gain, weights, input_map, kept_hidden, kept_values, kept_features,
    following, hidden_out, values_out, features_out, normed, activated,
):
    active, first, last = (flags[0], flags[1], flags[2])
    width = incoming.shape[1]

    @pl.when(active == 1)
    def _():
        hidden = jnp.where(first == 1, entry[0], incoming[...])
        hidden_out[0] = hidden
        widened = hidden.astype(f32)
        normed[...] = (widened * inverse_root(widened) * gain[...].astype(f32)).astype(bf16)
        values = jnp.dot(normed[...], weights[0], preferred_element_type=f32)
        values_out[0] = values
        activated[...] = (values * jax.nn.sigmoid(values)).astype(bf16)

        @pl.when(last == 0)
        def _():
            for at in range(0, width, CHUNK):
                branch = lax.dot_general(
                    activated[...], weights[1, at : at + CHUNK, :], NT, preferred_element_type=f32
                )
                kept = hidden_out[0, :, at : at + CHUNK].astype(f32)
                following[:, at : at + CHUNK] = (kept + branch).astype(bf16)

        features_out[0] = lax.dot_general(
            normed[...], input_map[...], NT, preferred_element_type=f32
        ).astype(bf16)


def backward_kernel(
    flags, entry, incoming, kept_hidden, kept_values, kept_features, gain, weights, output_map,
    kept_grads, previous, grads_out, weighted, slopes,
):
    active, first, last = (flags[0], flags[1], flags[2])
    rows, width = incoming.shape

    @pl.when(active == 1)
    def _():
        cotangent = jnp.where(last == 1, entry[0], incoming[...])
        upstream = jnp.dot(cotangent, weights[1], preferred_element_type=f32)
        values = kept_values[0]
        logistic = jax.nn.sigmoid(values)
        slopes[...] = (upstream * logistic * (1.0 + values * (1.0 - logistic))).astype(bf16)

        @pl.when(first == 0)
        def _():
            widened = kept_hidden[0].astype(f32)
            factor = inverse_root(widened)
            inner = jnp.zeros((rows, 1), f32)
            for at in range(0, width, CHUNK):
                part = lax.dot_general(
                    slopes[...], weights[0, at : at + CHUNK, :], NT, preferred_element_type=f32
                ) * gain[:, at : at + CHUNK].astype(f32)
                weighted[:, at : at + CHUNK] = part
                inner += jnp.sum(
                    part * kept_hidden[0, :, at : at + CHUNK].astype(f32), axis=-1, keepdims=True
                )
            pull = (factor * factor * factor) * (inner / width)
            for at in range(0, width, CHUNK):
                span = slice(at, at + CHUNK)
                arrived = jnp.where(last == 1, entry[0, :, span], incoming[:, span]).astype(f32)
                hidden_grad = factor * weighted[:, span] - kept_hidden[0, :, span].astype(f32) * pull
                previous[:, span] = (arrived + hidden_grad).astype(bf16)

        signals = lax.dot_general(
            slopes[...], output_map[...], NT, preferred_element_type=f32
        ).astype(bf16)
        grads_out[0] = (
            lax.dot_general(signals, kept_features[0], TN, preferred_element_type=f32) / rows
        )


def scores_kernel(every, own, inverse, select, out):
    count = every.shape[0]
    queries = select.shape[1]
    against = exact_dot(every[...], inverse[...])
    gram = -lax.dot_general(
        against, every[...], NT, precision=EXACT, preferred_element_type=f32
    )
    eye = (
        lax.broadcasted_iota(jnp.int32, (count, count), 0)
        == lax.broadcasted_iota(jnp.int32, (count, count), 1)
    ).astype(f32)
    solved = -exact_dot(swept(gram + eye), exact_dot(gram, select[...]))
    out[...] = exact_dot(own[...], solved)


def per_device(
    inputs,
    output_cotangent,
    lengths,
    query_examples,
    norm_gain,
    value_weight,
    output_weight,
    input_projection,
    output_projection,
    fisher_prior,
):
    sections = lax.axis_size("section")
    section = lax.axis_index("section")
    both = jnp.concatenate([value_weight, output_weight], axis=0)
    weights = lax.all_gather(both, "dp", axis=1, tiled=True)
    inverse = minus_inverse(fisher_prior[0])
    weights = pltpu.with_memory_space_constraint(weights, pltpu.VMEM)
    input_map = input_projection[0]
    output_map = output_projection[0]
    batches = lengths.shape[0]
    rows = inputs.shape[0] // batches
    width = inputs.shape[1]
    inner = weights.shape[2]
    features = input_map.shape[0]
    signals = output_map.shape[0]
    entries = inputs.reshape(batches, rows, width)
    positions = jnp.arange(rows, dtype=jnp.int32)
    keep = (positions[None, :] < lengths[:, None]).astype(bf16)
    targets = output_cotangent.reshape(batches, rows, width) * keep[:, :, None]
    first = (section == 0).astype(jnp.int32)
    last = (section == sections - 1).astype(jnp.int32)

    def flags_at(turn):
        active = (turn >= 0) & (turn < batches)
        entry = jnp.clip(turn, 0, batches - 1)
        slot = jnp.where(active, turn, batches)
        return jnp.stack([active.astype(jnp.int32), first, last, slot, entry]).astype(jnp.int32)

    def slotted(shape):
        return pl.BlockSpec((1, *shape), lambda _, flags: (flags[3], 0, 0))

    def entering():
        return pl.BlockSpec((1, rows, width), lambda _, flags: (flags[4], 0, 0))

    untouched = pl.BlockSpec(memory_space=pl.ANY)
    flops = 4 * rows * width * inner
    cost = pl.CostEstimate(flops=flops, bytes_accessed=4 * width * inner, transcendentals=0)

    def forward(flags, incoming, state):
        shapes = ((rows, width), (rows, inner), (rows, features))
        following, *state = pl.pallas_call(
            forward_kernel,
            grid_spec=pltpu.PrefetchScalarGridSpec(
                num_scalar_prefetch=1,
                grid=(1,),
                in_specs=[entering(), whole(), whole(), whole(), whole()] + [untouched] * 3,
                out_specs=[whole()] + [slotted(shape) for shape in shapes],
                scratch_shapes=[pltpu.VMEM((rows, width), bf16), pltpu.VMEM((rows, inner), bf16)],
            ),
            out_shape=[jax.ShapeDtypeStruct((rows, width), bf16)]
            + [jax.ShapeDtypeStruct(s.shape, s.dtype) for s in state],
            input_output_aliases={6: 1, 7: 2, 8: 3},
            compiler_params=pltpu.CompilerParams(vmem_limit_bytes=24 * MEBI),
            cost_estimate=cost,
            name="forward_block",
        )(flags, entries, incoming, norm_gain, weights, input_map, *state)
        return following, state

    def backward(flags, incoming, state, grads):
        return pl.pallas_call(
            backward_kernel,
            grid_spec=pltpu.PrefetchScalarGridSpec(
                num_scalar_prefetch=1,
                grid=(1,),
                in_specs=[
                    entering(), whole(), slotted((rows, width)), slotted((rows, inner)),
                    slotted((rows, features)), whole(), whole(), whole(), untouched,
                ],
                out_specs=[whole(), slotted((signals, features))],
                scratch_shapes=[pltpu.VMEM((rows, width), f32), pltpu.VMEM((rows, inner), bf16)],
            ),
            out_shape=[
                jax.ShapeDtypeStruct((rows, width), bf16),
                jax.ShapeDtypeStruct(grads.shape, grads.dtype),
            ],
            input_output_aliases={9: 1},
            compiler_params=pltpu.CompilerParams(vmem_limit_bytes=24 * MEBI),
            cost_estimate=cost,
            name="backward_block",
        )(flags, targets, incoming, *state, norm_gain, weights, output_map, grads)

    slots = batches + 1
    state = (
        jnp.zeros((slots, rows, width), bf16),
        jnp.zeros((slots, rows, inner), f32),
        jnp.zeros((slots, rows, features), bf16),
    )
    grads = jnp.zeros((slots, signals, features), f32)
    up = jnp.zeros((rows, width), bf16)
    down = jnp.zeros((rows, width), bf16)
    for tick in range(2 * sections + batches - 1):
        stages = [tick - m for m in range(batches)]
        back = [s for s in stages if sections <= s < 2 * sections]
        ahead = [s for s in stages if 0 <= s < sections]
        if back:
            down, grads = backward(flags_at(tick - (2 * sections - 1 - section)), down, state, grads)
            pairs = [(2 * sections - 1 - s, 2 * sections - 2 - s) for s in back if s < 2 * sections - 1]
            if pairs:
                down = lax.ppermute(down, "section", pairs)
        if ahead:
            up, state = forward(flags_at(tick - section), up, state)
            pairs = [(s, s + 1) for s in ahead if s < sections - 1]
            if pairs:
                up = lax.ppermute(up, "section", pairs)

    flat = grads[:batches].reshape(batches, signals * features)
    everyone = lax.all_to_all(
        jnp.broadcast_to(flat[None], (lax.axis_size("dp"), *flat.shape)), "dp", 0, 0, tiled=True
    ).reshape(-1, flat.shape[1])
    owners = jnp.arange(everyone.shape[0], dtype=jnp.int32)
    select = (owners[:, None] == query_examples[None, :]).astype(f32)
    mine = lax.axis_index("dp") * batches + jnp.arange(batches, dtype=jnp.int32)
    own = (mine[:, None] == owners[None, :]).astype(f32)
    section_scores = pl.pallas_call(
        scores_kernel,
        out_shape=jax.ShapeDtypeStruct((batches, select.shape[1]), f32),
        in_specs=[whole()] * 4,
        out_specs=whole(),
        compiler_params=pltpu.CompilerParams(vmem_limit_bytes=24 * MEBI),
        name="section_scores",
    )(everyone, own, inverse, select)
    shares = lax.all_to_all(
        jnp.broadcast_to(section_scores[None], (sections, *section_scores.shape)),
        "section", 0, 0, tiled=True,
    )
    return shares.sum(axis=0)


def solution(mesh):
    placed = (
        P("dp", None),
        P("dp", None),
        P("dp"),
        P(),
        P("section", None),
        P("section", "dp", None),
        P("section", "dp", None),
        P("section", None, None),
        P("section", None, None),
        P("section", None, None),
    )
    return jax.shard_map(
        per_device, mesh=mesh, in_specs=placed, out_specs=P("dp", None), check_vma=False
    )
```

```python
import functools

import jax
import jax.numpy as jnp
from jax import lax
from jax.experimental import pallas as pl
from jax.experimental.pallas import tpu as pltpu
from jax.sharding import PartitionSpec as P

EXACT = lax.Precision.HIGHEST
BLOCK = 128
CHUNK = 512
f32 = jnp.float32
bf16 = jnp.bfloat16
NT = (((1,), (1,)), ((), ()))
TN = (((0,), (0,)), ((), ()))
MEBI = 1 << 20


def whole():
    return pl.BlockSpec(memory_space=pltpu.VMEM)


def swept(block):
    size = block.shape[0]
    lanes = lax.broadcasted_iota(jnp.int32, (1, size), 1)
    rows = lax.broadcasted_iota(jnp.int32, (size, 1), 0)
    for at in range(size):
        column = block[:, at : at + 1]
        row = block[at : at + 1, :]
        inverse = 1.0 / column[at : at + 1, :]
        scaled = jnp.where(lanes == at, -inverse, row * inverse)
        column = jnp.where(rows == at, -1.0, column)
        kept = jnp.where((lanes == at) | (rows == at), 0.0, block)
        block = kept - column * scaled
    return block


def exact_dot(a, b):
    return jnp.dot(a, b, precision=EXACT, preferred_element_type=f32)


def inverse_kernel(prior, out):
    size = prior.shape[0]
    tall = min(256, size)
    out[...] = prior[...]

    def step(turn, _):
        span = pl.ds(pl.multiple_of(turn * BLOCK, BLOCK), BLOCK)
        pivot = swept(out[span, span])
        left = out[:, span]
        above = out[span, :]
        right = -exact_dot(left, pivot)
        below = -exact_dot(pivot, above)
        for row in range(0, size, tall):
            out[row : row + tall, :] -= exact_dot(right[row : row + tall], above)
        out[:, span] = right
        out[span, :] = below
        out[span, span] = pivot
        return 0

    lax.fori_loop(0, size // BLOCK, step, 0)


def minus_inverse(prior):
    size = prior.shape[0]
    return pl.pallas_call(
        inverse_kernel,
        out_shape=jax.ShapeDtypeStruct(prior.shape, f32),
        in_specs=[whole()],
        out_specs=whole(),
        compiler_params=pltpu.CompilerParams(vmem_limit_bytes=32 * MEBI),
        cost_estimate=pl.CostEstimate(
            flops=60 * size**3, bytes_accessed=8 * size * size, transcendentals=0
        ),
        name="prior_inverse",
    )(prior)


def inverse_root(hidden):
    return lax.rsqrt(jnp.mean(hidden * hidden, axis=-1, keepdims=True) + 1e-05)


def moved(source, target, arrived, at):
    copy = pltpu.make_async_copy(source, target, arrived.at[at])
    copy.start()
    return copy


def load_kernel(source, target, arrived):
    moved(source, target, arrived, 0).wait()


def forward_kernel(
    tick, batches, sections, entries, incoming, gain, weights, input_map, kept_hidden, kept_values,
    kept_features, following, hiddens, values_out, features_out,
    hidden, normed, values, activated, features, outgoing, arrived,
):
    section = lax.axis_index("section")
    turn = tick - section
    width = incoming.shape[1]

    @pl.when((turn >= 0) & (turn < batches))
    def _():
        @pl.when(section == 0)
        def _():
            moved(entries.at[turn], hidden, arrived, 0).wait()

        @pl.when(section != 0)
        def _():
            moved(incoming, hidden, arrived, 0).wait()

        saves = [moved(hidden, hiddens.at[turn], arrived, 1)]
        widened = hidden[...].astype(f32)
        normed[...] = (widened * inverse_root(widened) * gain[...].astype(f32)).astype(bf16)
        values[...] = jnp.dot(normed[...], weights[0], preferred_element_type=f32)
        saves.append(moved(values, values_out.at[turn], arrived, 2))
        activated[...] = (values[...] * jax.nn.sigmoid(values[...])).astype(bf16)

        @pl.when(section != sections - 1)
        def _():
            sent = []
            for at in range(0, width, CHUNK):
                span = pl.ds(at, CHUNK)
                branch = lax.dot_general(
                    activated[...], weights[1, span, :], NT, preferred_element_type=f32
                )
                outgoing[:, span] = (hidden[:, span].astype(f32) + branch).astype(bf16)
                sent.append(
                    moved(outgoing.at[:, span], following.at[:, span], arrived, 4 + at // CHUNK)
                )
            for copy in sent:
                copy.wait()

        features[...] = lax.dot_general(
            normed[...], input_map[...], NT, preferred_element_type=f32
        ).astype(bf16)
        saves.append(moved(features, features_out.at[turn], arrived, 3))
        for copy in saves:
            copy.wait()


def backward_kernel(
    tick, batches, sections, entries, incoming, hiddens, values_in, features_in, gain, weights,
    output_map, kept_grads, previous, grads_out,
    cotangent, hidden, values, features, weighted, slopes, outgoing, grads, arrived,
):
    section = lax.axis_index("section")
    turn = tick - (2 * sections - 1 - section)
    rows, width = incoming.shape

    @pl.when((turn >= 0) & (turn < batches))
    def _():
        values_here = moved(values_in.at[turn], values, arrived, 1)
        hidden_here = moved(hiddens.at[turn], hidden, arrived, 2)
        features_here = moved(features_in.at[turn], features, arrived, 3)

        @pl.when(section == sections - 1)
        def _():
            moved(entries.at[turn], cotangent, arrived, 0).wait()

        @pl.when(section != sections - 1)
        def _():
            moved(incoming, cotangent, arrived, 0).wait()

        upstream = jnp.dot(cotangent[...], weights[1], preferred_element_type=f32)
        values_here.wait()
        hidden_here.wait()
        features_here.wait()
        logistic = jax.nn.sigmoid(values[...])
        slopes[...] = (
            upstream * logistic * (1.0 + values[...] * (1.0 - logistic))
        ).astype(bf16)

        @pl.when(section != 0)
        def _():
            widened = hidden[...].astype(f32)
            factor = inverse_root(widened)
            inner = jnp.zeros((rows, 1), f32)
            for at in range(0, width, CHUNK):
                span = pl.ds(at, CHUNK)
                part = lax.dot_general(
                    slopes[...], weights[0, span, :], NT, preferred_element_type=f32
                ) * gain[:, span].astype(f32)
                weighted[:, span] = part
                inner += jnp.sum(part * hidden[:, span].astype(f32), axis=-1, keepdims=True)
            pull = (factor * factor * factor) * (inner / width)
            sent = []
            for at in range(0, width, CHUNK):
                span = pl.ds(at, CHUNK)
                hidden_grad = factor * weighted[:, span] - hidden[:, span].astype(f32) * pull
                outgoing[:, span] = (cotangent[:, span].astype(f32) + hidden_grad).astype(bf16)
                sent.append(
                    moved(outgoing.at[:, span], previous.at[:, span], arrived, 5 + at // CHUNK)
                )
            for copy in sent:
                copy.wait()

        signals = lax.dot_general(
            slopes[...], output_map[...], NT, preferred_element_type=f32
        ).astype(bf16)
        grads[...] = lax.dot_general(signals, features[...], TN, preferred_element_type=f32) / rows
        moved(grads, grads_out.at[turn], arrived, 4).wait()


def scores_kernel(every, own, inverse, select, out):
    count = every.shape[0]
    queries = select.shape[1]
    against = exact_dot(every[...], inverse[...])
    gram = -lax.dot_general(
        against, every[...], NT, precision=EXACT, preferred_element_type=f32
    )
    eye = (
        lax.broadcasted_iota(jnp.int32, (count, count), 0)
        == lax.broadcasted_iota(jnp.int32, (count, count), 1)
    ).astype(f32)
    solved = -exact_dot(swept(gram + eye), exact_dot(gram, select[...]))
    out[...] = exact_dot(own[...], solved)


def per_device(
    inputs,
    output_cotangent,
    lengths,
    query_examples,
    norm_gain,
    value_weight,
    output_weight,
    input_projection,
    output_projection,
    fisher_prior,
):
    sections = lax.axis_size("section")
    batches = lengths.shape[0]
    rows = inputs.shape[0] // batches
    width = inputs.shape[1]
    inner = value_weight.shape[2]
    features = input_projection.shape[1]
    signals = output_projection.shape[1]
    both = jnp.concatenate([value_weight, output_weight], axis=0)
    weights = lax.all_gather(both, "dp", axis=1, tiled=True)
    entries = inputs.reshape(batches, rows, width)
    positions = jnp.arange(rows, dtype=jnp.int32)
    keep = (positions[None, :] < lengths[:, None]).astype(bf16)
    targets = output_cotangent.reshape(batches, rows, width) * keep[:, :, None]
    state = (
        jnp.zeros((batches, rows, width), bf16),
        jnp.zeros((batches, rows, inner), f32),
        jnp.zeros((batches, rows, features), bf16),
    )
    grads = jnp.zeros((batches, signals, features), f32)
    empty = jnp.zeros((rows, width), bf16)
    weights, inverse, targets, state, grads, empty = lax.optimization_barrier(
        (weights, minus_inverse(fisher_prior[0]), targets, state, grads, empty)
    )
    far = pl.BlockSpec(memory_space=pltpu.HBM)
    weights = pltpu.with_memory_space_constraint(
        pl.pallas_call(
            load_kernel,
            out_shape=pltpu.VMEM(weights.shape, weights.dtype),
            in_specs=[far],
            out_specs=whole(),
            scratch_shapes=[pltpu.SemaphoreType.DMA((1,))],
            compiler_params=pltpu.CompilerParams(vmem_limit_bytes=40 * MEBI),
            name="weights_load",
        )(weights),
        pltpu.VMEM,
    )
    pieces = width // CHUNK
    block = jax.ShapeDtypeStruct((rows, width), bf16)
    cost = pl.CostEstimate(
        flops=4 * rows * width * inner, bytes_accessed=4 * width * inner, transcendentals=0
    )

    def like(*arrays):
        return [jax.ShapeDtypeStruct(a.shape, a.dtype) for a in arrays]

    def forward(tick, incoming, state):
        following, *state = pl.pallas_call(
            functools.partial(forward_kernel, tick, batches, sections),
            in_specs=[far, far, whole(), whole(), whole(), far, far, far],
            out_specs=[far, far, far, far],
            scratch_shapes=[
                pltpu.VMEM((rows, width), bf16),
                pltpu.VMEM((rows, width), bf16),
                pltpu.VMEM((rows, inner), f32),
                pltpu.VMEM((rows, inner), bf16),
                pltpu.VMEM((rows, features), bf16),
                pltpu.VMEM((rows, width), bf16),
                pltpu.SemaphoreType.DMA((4 + pieces,)),
            ],
            out_shape=[block, *like(*state)],
            input_output_aliases={5: 1, 6: 2, 7: 3},
            compiler_params=pltpu.CompilerParams(vmem_limit_bytes=16 * MEBI),
            cost_estimate=cost,
            name="forward_block",
        )(entries, incoming, norm_gain, weights, input_projection[0], *state)
        return following, state

    def backward(tick, incoming, grads):
        return pl.pallas_call(
            functools.partial(backward_kernel, tick, batches, sections),
            in_specs=[far] * 5 + [whole(), whole(), whole(), far],
            out_specs=[far, far],
            scratch_shapes=[
                pltpu.VMEM((rows, width), bf16),
                pltpu.VMEM((rows, width), bf16),
                pltpu.VMEM((rows, inner), f32),
                pltpu.VMEM((rows, features), bf16),
                pltpu.VMEM((rows, width), f32),
                pltpu.VMEM((rows, inner), bf16),
                pltpu.VMEM((rows, width), bf16),
                pltpu.VMEM((signals, features), f32),
                pltpu.SemaphoreType.DMA((5 + pieces,)),
            ],
            out_shape=[block, *like(grads)],
            input_output_aliases={8: 1},
            compiler_params=pltpu.CompilerParams(vmem_limit_bytes=16 * MEBI),
            cost_estimate=cost,
            name="backward_block",
        )(targets, incoming, *state, norm_gain, weights, output_projection[0], grads)

    up = empty
    down = empty
    for tick in range(2 * sections + batches - 1):
        stages = [tick - m for m in range(batches)]
        back = [s for s in stages if sections <= s < 2 * sections]
        ahead = [s for s in stages if 0 <= s < sections]
        if back:
            down, grads = backward(tick, down, grads)
            pairs = [(2 * sections - 1 - s, 2 * sections - 2 - s) for s in back if s < 2 * sections - 1]
            if pairs:
                down = lax.ppermute(down, "section", pairs)
        if ahead:
            up, state = forward(tick, up, state)
            pairs = [(s, s + 1) for s in ahead if s < sections - 1]
            if pairs:
                up = lax.ppermute(up, "section", pairs)

    flat = grads.reshape(batches, signals * features)
    everyone = lax.all_to_all(
        jnp.broadcast_to(flat[None], (lax.axis_size("dp"), *flat.shape)), "dp", 0, 0, tiled=True
    ).reshape(-1, flat.shape[1])
    owners = jnp.arange(everyone.shape[0], dtype=jnp.int32)
    select = (owners[:, None] == query_examples[None, :]).astype(f32)
    mine = lax.axis_index("dp") * batches + jnp.arange(batches, dtype=jnp.int32)
    own = (mine[:, None] == owners[None, :]).astype(f32)
    section_scores = pl.pallas_call(
        scores_kernel,
        out_shape=jax.ShapeDtypeStruct((batches, select.shape[1]), f32),
        in_specs=[whole()] * 4,
        out_specs=whole(),
        compiler_params=pltpu.CompilerParams(vmem_limit_bytes=24 * MEBI),
        name="section_scores",
    )(everyone, own, inverse, select)
    shares = lax.all_to_all(
        jnp.broadcast_to(section_scores[None], (sections, *section_scores.shape)),
        "section", 0, 0, tiled=True,
    )
    return shares.sum(axis=0)


def solution(mesh):
    placed = (
        P("dp", None),
        P("dp", None),
        P("dp"),
        P(),
        P("section", None),
        P("section", "dp", None),
        P("section", "dp", None),
        P("section", None, None),
        P("section", None, None),
        P("section", None, None),
    )
    return jax.shard_map(
        per_device, mesh=mesh, in_specs=placed, out_specs=P("dp", None), check_vma=False
    )
```

```python
import functools

import jax
import jax.numpy as jnp
from jax import lax
from jax.experimental import pallas as pl
from jax.experimental.pallas import tpu as pltpu
from jax.sharding import PartitionSpec as P

EXACT = lax.Precision.HIGHEST
BLOCK = 128
CHUNK = 512
WIDE = 256
TILE = 128
f32 = jnp.float32
bf16 = jnp.bfloat16
NT = (((1,), (1,)), ((), ()))
TN = (((0,), (0,)), ((), ()))
MEBI = 1 << 20


def whole():
    return pl.BlockSpec(memory_space=pltpu.VMEM)


def swept(block):
    size = block.shape[0]
    lanes = lax.broadcasted_iota(jnp.int32, (1, size), 1)
    rows = lax.broadcasted_iota(jnp.int32, (size, 1), 0)
    for at in range(size):
        column = block[:, at : at + 1]
        row = block[at : at + 1, :]
        inverse = 1.0 / column[at : at + 1, :]
        scaled = jnp.where(lanes == at, -inverse, row * inverse)
        column = jnp.where(rows == at, -1.0, column)
        kept = jnp.where((lanes == at) | (rows == at), 0.0, block)
        block = kept - column * scaled
    return block


def exact_dot(a, b):
    return jnp.dot(a, b, precision=EXACT, preferred_element_type=f32)


def inverse_kernel(prior, out):
    size = prior.shape[0]
    tall = min(256, size)
    out[...] = prior[...]

    def step(turn, _):
        span = pl.ds(pl.multiple_of(turn * BLOCK, BLOCK), BLOCK)
        pivot = swept(out[span, span])
        left = out[:, span]
        above = out[span, :]
        right = -exact_dot(left, pivot)
        below = -exact_dot(pivot, above)
        for row in range(0, size, tall):
            out[row : row + tall, :] -= exact_dot(right[row : row + tall], above)
        out[:, span] = right
        out[span, :] = below
        out[span, span] = pivot
        return 0

    lax.fori_loop(0, size // BLOCK, step, 0)


def minus_inverse(prior):
    size = prior.shape[0]
    return pl.pallas_call(
        inverse_kernel,
        out_shape=jax.ShapeDtypeStruct(prior.shape, f32),
        in_specs=[whole()],
        out_specs=whole(),
        compiler_params=pltpu.CompilerParams(vmem_limit_bytes=32 * MEBI),
        cost_estimate=pl.CostEstimate(
            flops=60 * size**3, bytes_accessed=8 * size * size, transcendentals=0
        ),
        name="prior_inverse",
    )(prior)


def inverse_root(hidden):
    return lax.rsqrt(jnp.mean(hidden * hidden, axis=-1, keepdims=True) + 1e-05)


def moved(source, target, arrived, at):
    copy = pltpu.make_async_copy(source, target, arrived.at[at])
    copy.start()
    return copy


def nothing_kernel(*targets):
    pass


def load_kernel(source, target, arrived):
    moved(source, target, arrived, 0).wait()


def tiles_joined(tiles, at):
    return jnp.concatenate(
        [
            jnp.concatenate(
                [
                    tiles[pl.ds(pl.multiple_of(at + across, TILE), TILE), down : down + TILE]
                    for down in range(0, tiles.shape[1], TILE)
                ],
                axis=0,
            )
            for across in range(0, CHUNK, TILE)
        ],
        axis=1,
    )


def turned_kernel(low, high, sides, source, target):
    section = lax.axis_index("section")

    @pl.when((section >= low) & (section < high))
    def _():
        def strip(at, _):
            rows = pl.ds(pl.multiple_of(at * TILE, TILE), TILE)
            for side in sides:
                for column in range(0, source.shape[2], TILE):
                    span = slice(column, column + TILE)
                    target[side, rows, span] = source[side, rows, span].T
            return 0

        lax.fori_loop(0, source.shape[1] // TILE, strip, 0)


def forward_kernel(
    tick, batches, sections, entries, incoming, gain, weights, input_map, kept_hidden, kept_values,
    kept_features, following, hiddens, values_out, features_out,
    hidden, normed, values, activated, features, outgoing, arrived,
):
    section = lax.axis_index("section")
    turn = tick - section
    width = incoming.shape[1]

    @pl.when((turn >= 0) & (turn < batches))
    def _():
        @pl.when(section == 0)
        def _():
            moved(entries.at[turn], hidden, arrived, 0).wait()

        @pl.when(section != 0)
        def _():
            moved(incoming, hidden, arrived, 0).wait()

        saves = [moved(hidden, hiddens.at[turn], arrived, 1)]
        widened = hidden[...].astype(f32)
        normed[...] = (widened * inverse_root(widened) * gain[...].astype(f32)).astype(bf16)

        def inward(at, _):
            span = pl.ds(pl.multiple_of(at * WIDE, WIDE), WIDE)
            part = jnp.dot(normed[...], weights[0, :, span], preferred_element_type=f32)
            values[:, span] = part
            activated[:, span] = (part * jax.nn.sigmoid(part)).astype(bf16)
            return 0

        lax.fori_loop(0, weights.shape[2] // WIDE, inward, 0)
        saves.append(moved(values, values_out.at[turn], arrived, 2))

        @pl.when(section != sections - 1)
        def _():
            def outward(at, _):
                start = pl.multiple_of(at * CHUNK, CHUNK)
                span = pl.ds(start, CHUNK)
                branch = jnp.dot(
                    activated[...], tiles_joined(weights.at[1], start), preferred_element_type=f32
                )
                outgoing[:, span] = (hidden[:, span].astype(f32) + branch).astype(bf16)
                return 0

            lax.fori_loop(0, width // CHUNK, outward, 0)
            moved(outgoing, following, arrived, 4).wait()

        features[...] = lax.dot_general(
            normed[...], input_map[...], NT, preferred_element_type=f32
        ).astype(bf16)
        saves.append(moved(features, features_out.at[turn], arrived, 3))
        for copy in saves:
            copy.wait()


def backward_kernel(
    tick, batches, sections, entries, incoming, hiddens, values_in, features_in, gain, weights,
    output_map, kept_grads, previous, grads_out,
    cotangent, hidden, values, features, upstream, weighted, slopes, outgoing, grads, arrived,
):
    section = lax.axis_index("section")
    turn = tick - (2 * sections - 1 - section)
    rows, width = incoming.shape

    @pl.when((turn >= 0) & (turn < batches))
    def _():
        values_here = moved(values_in.at[turn], values, arrived, 1)
        hidden_here = moved(hiddens.at[turn], hidden, arrived, 2)
        features_here = moved(features_in.at[turn], features, arrived, 3)

        @pl.when(section == sections - 1)
        def _():
            moved(entries.at[turn], cotangent, arrived, 0).wait()

        @pl.when(section != sections - 1)
        def _():
            moved(incoming, cotangent, arrived, 0).wait()

        values_here.wait()
        hidden_here.wait()
        features_here.wait()

        @pl.when(section == sections - 2)
        def _():
            def gathered(at, _):
                span = pl.ds(pl.multiple_of(at * CHUNK, CHUNK), CHUNK)
                upstream[...] += lax.dot_general(
                    cotangent[:, span],
                    tiles_joined(weights.at[1], at * CHUNK),
                    NT,
                    preferred_element_type=f32,
                )
                return 0

            upstream[...] = jnp.zeros_like(upstream)
            lax.fori_loop(0, width // CHUNK, gathered, 0)

        @pl.when(section != sections - 2)
        def _():
            def inward(at, _):
                span = pl.ds(pl.multiple_of(at * WIDE, WIDE), WIDE)
                upstream[:, span] = jnp.dot(
                    cotangent[...], weights[1, :, span], preferred_element_type=f32
                )
                return 0

            lax.fori_loop(0, weights.shape[2] // WIDE, inward, 0)

        here = values[...]
        logistic = jax.nn.sigmoid(here)
        slopes[...] = (upstream[...] * logistic * (1.0 + here * (1.0 - logistic))).astype(bf16)

        def outward(product):
            widened = hidden[...].astype(f32)
            factor = inverse_root(widened)

            def piece(at, inner):
                start = pl.multiple_of(at * CHUNK, CHUNK)
                span = pl.ds(start, CHUNK)
                part = product(start) * gain[:, span].astype(f32)
                weighted[:, span] = part
                return inner + jnp.sum(
                    part * hidden[:, span].astype(f32), axis=-1, keepdims=True
                )

            inner = lax.fori_loop(0, width // CHUNK, piece, jnp.zeros((rows, 1), f32))
            pull = (factor * factor * factor) * (inner / width)
            hidden_grad = factor * weighted[...] - hidden[...].astype(f32) * pull
            outgoing[...] = (cotangent[...].astype(f32) + hidden_grad).astype(bf16)
            moved(outgoing, previous, arrived, 5).wait()

        @pl.when(section >= sections - 2)
        def _():
            outward(
                lambda start: lax.dot_general(
                    slopes[...], weights[0, pl.ds(start, CHUNK), :], NT, preferred_element_type=f32
                )
            )

        @pl.when((section != 0) & (section < sections - 2))
        def _():
            outward(
                lambda start: jnp.dot(
                    slopes[...], tiles_joined(weights.at[0], start), preferred_element_type=f32
                )
            )

        signals = lax.dot_general(
            slopes[...], output_map[...], NT, preferred_element_type=f32
        ).astype(bf16)
        grads[...] = lax.dot_general(signals, features[...], TN, preferred_element_type=f32) / rows
        moved(grads, grads_out.at[turn], arrived, 4).wait()


def scores_kernel(queries, every, inverse, out):
    count = every.shape[0]
    batches, chosen = out.shape
    against = exact_dot(every[...], inverse[...])
    gram = -lax.dot_general(
        against, every[...], NT, precision=EXACT, preferred_element_type=f32
    )

    def counted(shape, axis):
        return lax.broadcasted_iota(jnp.int32, shape, axis)

    eye = (counted((count, count), 0) == counted((count, count), 1)).astype(f32)
    select = (counted((count, chosen), 0) == queries[...]).astype(f32)
    solved = -exact_dot(swept(gram + eye), exact_dot(gram, select))
    mine = lax.axis_index("dp") * batches + counted((batches, count), 0)
    own = (counted((batches, count), 1) == mine).astype(f32)
    out[...] = exact_dot(own, solved)


def per_device(
    inputs,
    output_cotangent,
    lengths,
    query_examples,
    norm_gain,
    value_weight,
    output_weight,
    input_projection,
    output_projection,
    fisher_prior,
):
    sections = lax.axis_size("section")
    batches = lengths.shape[0]
    rows = inputs.shape[0] // batches
    width = inputs.shape[1]
    inner = value_weight.shape[2]
    features = input_projection.shape[1]
    signals = output_projection.shape[1]
    held = value_weight.shape[1]
    turned = output_weight.reshape(held // TILE, TILE, inner // TILE, TILE)
    turned = turned.transpose(0, 3, 2, 1).reshape(output_weight.shape)
    both = jnp.concatenate([value_weight, turned], axis=0)
    weights = lax.all_gather(both, "dp", axis=1, tiled=True)
    entries = inputs.reshape(batches, rows, width)
    positions = jnp.arange(rows, dtype=jnp.int32)
    keep = (positions[None, :] < lengths[:, None]).astype(bf16)
    targets = output_cotangent.reshape(batches, rows, width) * keep[:, :, None]
    kinds = (
        ((batches, rows, width), bf16),
        ((batches, rows, inner), f32),
        ((batches, rows, features), bf16),
        ((batches, signals, features), f32),
        ((rows, width), bf16),
    )
    *state, grads, empty = pl.pallas_call(
        nothing_kernel,
        out_shape=[jax.ShapeDtypeStruct(*kind) for kind in kinds],
        out_specs=[whole()] * len(kinds),
        compiler_params=pltpu.CompilerParams(vmem_limit_bytes=8 * MEBI),
        name="room",
    )()
    weights, inverse, targets = lax.optimization_barrier(
        (weights, minus_inverse(fisher_prior[0]), targets)
    )
    far = pl.BlockSpec(memory_space=pltpu.HBM)
    weights = pltpu.with_memory_space_constraint(
        pl.pallas_call(
            load_kernel,
            out_shape=pltpu.VMEM(weights.shape, weights.dtype),
            in_specs=[far],
            out_specs=whole(),
            scratch_shapes=[pltpu.SemaphoreType.DMA((1,))],
            compiler_params=pltpu.CompilerParams(vmem_limit_bytes=40 * MEBI),
            name="weights_load",
        )(weights),
        pltpu.VMEM,
    )
    block = jax.ShapeDtypeStruct((rows, width), bf16)

    def turned_again(low, high, sides, weights):
        again = pl.pallas_call(
            functools.partial(turned_kernel, low, high, sides),
            out_shape=pltpu.VMEM(weights.shape, weights.dtype),
            in_specs=[whole()],
            out_specs=whole(),
            input_output_aliases={0: 0},
            compiler_params=pltpu.CompilerParams(vmem_limit_bytes=8 * MEBI),
            name="weights_turned",
        )(weights)
        return pltpu.with_memory_space_constraint(again, pltpu.VMEM)

    cost = pl.CostEstimate(
        flops=4 * rows * width * inner, bytes_accessed=4 * width * inner, transcendentals=0
    )

    def like(*arrays):
        return [jax.ShapeDtypeStruct(a.shape, a.dtype) for a in arrays]

    def forward(tick, incoming, weights, state):
        following, *state = pl.pallas_call(
            functools.partial(forward_kernel, tick, batches, sections),
            in_specs=[far, far, whole(), whole(), whole(), far, far, far],
            out_specs=[far, far, far, far],
            scratch_shapes=[
                pltpu.VMEM((rows, width), bf16),
                pltpu.VMEM((rows, width), bf16),
                pltpu.VMEM((rows, inner), f32),
                pltpu.VMEM((rows, inner), bf16),
                pltpu.VMEM((rows, features), bf16),
                pltpu.VMEM((rows, width), bf16),
                pltpu.SemaphoreType.DMA((5,)),
            ],
            out_shape=[block, *like(*state)],
            input_output_aliases={5: 1, 6: 2, 7: 3},
            compiler_params=pltpu.CompilerParams(vmem_limit_bytes=14 * MEBI),
            cost_estimate=cost,
            name="forward_block",
        )(entries, incoming, norm_gain, weights, input_projection[0], *state)
        return following, state

    def backward(tick, incoming, weights, grads):
        return pl.pallas_call(
            functools.partial(backward_kernel, tick, batches, sections),
            in_specs=[far] * 5 + [whole(), whole(), whole(), far],
            out_specs=[far, far],
            scratch_shapes=[
                pltpu.VMEM((rows, width), bf16),
                pltpu.VMEM((rows, width), bf16),
                pltpu.VMEM((rows, inner), f32),
                pltpu.VMEM((rows, features), bf16),
                pltpu.VMEM((rows, inner), f32),
                pltpu.VMEM((rows, width), f32),
                pltpu.VMEM((rows, inner), bf16),
                pltpu.VMEM((rows, width), bf16),
                pltpu.VMEM((signals, features), f32),
                pltpu.SemaphoreType.DMA((6,)),
            ],
            out_shape=[block, *like(grads)],
            input_output_aliases={8: 1},
            compiler_params=pltpu.CompilerParams(vmem_limit_bytes=16 * MEBI),
            cost_estimate=cost,
            name="backward_block",
        )(targets, incoming, *state, norm_gain, weights, output_projection[0], grads)

    weights = turned_again(sections - 1, sections, (1,), weights)
    up = empty
    down = empty
    for tick in range(2 * sections + batches - 1):
        stages = [tick - m for m in range(batches)]
        back = [s for s in stages if sections <= s < 2 * sections]
        ahead = [s for s in stages if 0 <= s < sections]
        if back:
            down, grads = backward(tick, down, weights, grads)
            pairs = [(2 * sections - 1 - s, 2 * sections - 2 - s) for s in back if s < 2 * sections - 1]
            if pairs:
                down = lax.ppermute(down, "section", pairs)
        if ahead:
            up, state = forward(tick, up, weights, state)
            pairs = [(s, s + 1) for s in ahead if s < sections - 1]
            if pairs:
                up = lax.ppermute(up, "section", pairs)
            if tick == sections + batches - 4:
                up, weights = lax.optimization_barrier((up, weights))
                weights = turned_again(0, sections - 2, (0, 1), weights)

    flat = grads.reshape(batches, signals * features)
    everyone = lax.all_to_all(
        jnp.broadcast_to(flat[None], (lax.axis_size("dp"), *flat.shape)), "dp", 0, 0, tiled=True
    ).reshape(-1, flat.shape[1])
    section_scores = pl.pallas_call(
        scores_kernel,
        out_shape=jax.ShapeDtypeStruct((batches, query_examples.shape[0]), f32),
        in_specs=[whole()] * 3,
        out_specs=whole(),
        compiler_params=pltpu.CompilerParams(vmem_limit_bytes=24 * MEBI),
        name="section_scores",
    )(query_examples[None], everyone, inverse)
    shares = lax.all_to_all(
        jnp.broadcast_to(section_scores[None], (sections, *section_scores.shape)),
        "section", 0, 0, tiled=True,
    )
    return shares.sum(axis=0)


def solution(mesh):
    placed = (
        P("dp", None),
        P("dp", None),
        P("dp"),
        P(),
        P("section", None),
        P("section", "dp", None),
        P("section", "dp", None),
        P("section", None, None),
        P("section", None, None),
        P("section", None, None),
    )
    return jax.shard_map(
        per_device, mesh=mesh, in_specs=placed, out_specs=P("dp", None), check_vma=False
    )
```

```python
import functools

import jax
import jax.numpy as jnp
from jax import lax
from jax.experimental import pallas as pl
from jax.experimental.pallas import tpu as pltpu
from jax.sharding import PartitionSpec as P

EXACT = lax.Precision.HIGHEST
BLOCK = 128
CHUNK = 1024
SPLIT = 2
f32 = jnp.float32
bf16 = jnp.bfloat16
NT = (((1,), (1,)), ((), ()))
TN = (((0,), (0,)), ((), ()))
MEBI = 1 << 20


def whole():
    return pl.BlockSpec(memory_space=pltpu.VMEM)


def swept(block):
    size = block.shape[0]
    lanes = lax.broadcasted_iota(jnp.int32, (1, size), 1)
    rows = lax.broadcasted_iota(jnp.int32, (size, 1), 0)
    for at in range(size):
        column = block[:, at : at + 1]
        row = block[at : at + 1, :]
        inverse = 1.0 / column[at : at + 1, :]
        scaled = jnp.where(lanes == at, -inverse, row * inverse)
        column = jnp.where(rows == at, -1.0, column)
        kept = jnp.where((lanes == at) | (rows == at), 0.0, block)
        block = kept - column * scaled
    return block


def exact_dot(a, b):
    return jnp.dot(a, b, precision=EXACT, preferred_element_type=f32)


def inverse_kernel(prior, out):
    size = prior.shape[0]
    tall = min(256, size)
    out[...] = prior[...]

    def step(turn, _):
        span = pl.ds(pl.multiple_of(turn * BLOCK, BLOCK), BLOCK)
        pivot = swept(out[span, span])
        left = out[:, span]
        above = out[span, :]
        right = -exact_dot(left, pivot)
        below = -exact_dot(pivot, above)
        for row in range(0, size, tall):
            out[row : row + tall, :] -= exact_dot(right[row : row + tall], above)
        out[:, span] = right
        out[span, :] = below
        out[span, span] = pivot
        return 0

    lax.fori_loop(0, size // BLOCK, step, 0)


def minus_inverse(prior):
    size = prior.shape[0]
    return pl.pallas_call(
        inverse_kernel,
        out_shape=jax.ShapeDtypeStruct(prior.shape, f32),
        in_specs=[whole()],
        out_specs=whole(),
        compiler_params=pltpu.CompilerParams(vmem_limit_bytes=32 * MEBI),
        cost_estimate=pl.CostEstimate(
            flops=60 * size**3, bytes_accessed=8 * size * size, transcendentals=0
        ),
        name="prior_inverse",
    )(prior)


def inverse_root(hidden):
    return lax.rsqrt(jnp.mean(hidden * hidden, axis=-1, keepdims=True) + 1e-05)


def moved(source, target, arrived, at):
    copy = pltpu.make_async_copy(source, target, arrived.at[at])
    copy.start()
    return copy


def nothing_kernel(*targets):
    pass


def load_kernel(source, target, arrived):
    moved(source, target, arrived, 0).wait()


def forward_kernel(
    tick, waves, sections, entries, incoming, gain, weights, input_map, kept_hidden, kept_values,
    kept_features, following, hiddens, values_out, features_out,
    hidden, normed, values, activated, features, arrived,
):
    section = lax.axis_index("section")
    turn = tick - section
    width = incoming.shape[1]

    @pl.when((turn >= 0) & (turn < waves))
    def _():
        @pl.when(section == 0)
        def _():
            moved(entries.at[turn], hidden, arrived, 0).wait()

        @pl.when(section != 0)
        def _():
            hidden[...] = incoming[...]

        saves = [moved(hidden, hiddens.at[turn], arrived, 1)]
        widened = hidden[...].astype(f32)
        normed[...] = (widened * inverse_root(widened) * gain[...].astype(f32)).astype(bf16)
        values[...] = jnp.dot(normed[...], weights[0], preferred_element_type=f32)
        saves.append(moved(values, values_out.at[turn], arrived, 2))
        activated[...] = (values[...] * jax.nn.sigmoid(values[...])).astype(bf16)

        @pl.when(section != sections - 1)
        def _():
            def outward(at, _):
                span = pl.ds(pl.multiple_of(at * CHUNK, CHUNK), CHUNK)
                branch = lax.dot_general(
                    activated[...], weights[1, span, :], NT, preferred_element_type=f32
                )
                following[:, span] = (hidden[:, span].astype(f32) + branch).astype(bf16)
                return 0

            lax.fori_loop(0, width // CHUNK, outward, 0)

        features[...] = lax.dot_general(
            normed[...], input_map[...], NT, preferred_element_type=f32
        ).astype(bf16)
        saves.append(moved(features, features_out.at[turn], arrived, 3))
        for copy in saves:
            copy.wait()


def backward_kernel(
    tick, waves, sections, entries, incoming, hiddens, values_in, features_in, gain, weights,
    output_map, kept_grads, previous, grads_out,
    cotangent, hidden, values, features, weighted, slopes, grads, arrived,
):
    section = lax.axis_index("section")
    turn = tick - (2 * sections - 1 - section)
    rows, width = incoming.shape

    @pl.when((turn >= 0) & (turn < waves))
    def _():
        values_here = moved(values_in.at[turn], values, arrived, 1)
        hidden_here = moved(hiddens.at[turn], hidden, arrived, 2)
        features_here = moved(features_in.at[turn], features, arrived, 3)

        @pl.when(section == sections - 1)
        def _():
            moved(entries.at[turn], cotangent, arrived, 0).wait()

        @pl.when(section != sections - 1)
        def _():
            cotangent[...] = incoming[...]

        upstream = jnp.dot(cotangent[...], weights[1], preferred_element_type=f32)
        values_here.wait()
        hidden_here.wait()
        features_here.wait()
        logistic = jax.nn.sigmoid(values[...])
        slopes[...] = (
            upstream * logistic * (1.0 + values[...] * (1.0 - logistic))
        ).astype(bf16)

        @pl.when(section != 0)
        def _():
            widened = hidden[...].astype(f32)
            factor = inverse_root(widened)

            def outward(at, inner):
                span = pl.ds(pl.multiple_of(at * CHUNK, CHUNK), CHUNK)
                part = lax.dot_general(
                    slopes[...], weights[0, span, :], NT, preferred_element_type=f32
                ) * gain[:, span].astype(f32)
                weighted[:, span] = part
                return inner + jnp.sum(
                    part * hidden[:, span].astype(f32), axis=-1, keepdims=True
                )

            inner = lax.fori_loop(0, width // CHUNK, outward, jnp.zeros((rows, 1), f32))
            pull = (factor * factor * factor) * (inner / width)
            hidden_grad = factor * weighted[...] - hidden[...].astype(f32) * pull
            previous[...] = (cotangent[...].astype(f32) + hidden_grad).astype(bf16)

        signals = lax.dot_general(
            slopes[...], output_map[...], NT, preferred_element_type=f32
        ).astype(bf16)
        grads[...] = lax.dot_general(signals, features[...], TN, preferred_element_type=f32)
        moved(grads, grads_out.at[turn], arrived, 4).wait()


def scores_kernel(queries, every, inverse, out):
    count = every.shape[0]
    batches, chosen = out.shape
    against = exact_dot(every[...], inverse[...])
    gram = -lax.dot_general(
        against, every[...], NT, precision=EXACT, preferred_element_type=f32
    )

    def counted(shape, axis):
        return lax.broadcasted_iota(jnp.int32, shape, axis)

    eye = (counted((count, count), 0) == counted((count, count), 1)).astype(f32)
    select = (counted((count, chosen), 0) == queries[...]).astype(f32)
    solved = -exact_dot(swept(gram + eye), exact_dot(gram, select))
    mine = lax.axis_index("dp") * batches + counted((batches, count), 0)
    own = (counted((batches, count), 1) == mine).astype(f32)
    out[...] = exact_dot(own, solved)


def per_device(
    inputs,
    output_cotangent,
    lengths,
    query_examples,
    norm_gain,
    value_weight,
    output_weight,
    input_projection,
    output_projection,
    fisher_prior,
):
    sections = lax.axis_size("section")
    batches = lengths.shape[0]
    length = inputs.shape[0] // batches
    waves = SPLIT * batches
    rows = length // SPLIT
    width = inputs.shape[1]
    inner = value_weight.shape[2]
    features = input_projection.shape[1]
    signals = output_projection.shape[1]
    both = jnp.concatenate([value_weight, output_weight], axis=0)
    weights = lax.all_gather(both, "dp", axis=1, tiled=True)
    entries = inputs.reshape(waves, rows, width)
    positions = jnp.arange(length, dtype=jnp.int32)
    keep = (positions[None, :] < lengths[:, None]).astype(bf16)
    targets = output_cotangent.reshape(batches, length, width) * keep[:, :, None]
    targets = targets.reshape(waves, rows, width)
    kinds = (
        ((waves, rows, width), bf16),
        ((waves, rows, inner), f32),
        ((waves, rows, features), bf16),
        ((waves, signals, features), f32),
        ((rows, width), bf16),
    )
    *state, grads, empty = pl.pallas_call(
        nothing_kernel,
        out_shape=[jax.ShapeDtypeStruct(*kind) for kind in kinds],
        out_specs=[whole()] * len(kinds),
        compiler_params=pltpu.CompilerParams(vmem_limit_bytes=8 * MEBI),
        name="room",
    )()
    weights, inverse, targets = lax.optimization_barrier(
        (weights, minus_inverse(fisher_prior[0]), targets)
    )
    far = pl.BlockSpec(memory_space=pltpu.HBM)
    weights = pltpu.with_memory_space_constraint(
        pl.pallas_call(
            load_kernel,
            out_shape=pltpu.VMEM(weights.shape, weights.dtype),
            in_specs=[far],
            out_specs=whole(),
            scratch_shapes=[pltpu.SemaphoreType.DMA((1,))],
            compiler_params=pltpu.CompilerParams(vmem_limit_bytes=40 * MEBI),
            name="weights_load",
        )(weights),
        pltpu.VMEM,
    )
    block = jax.ShapeDtypeStruct((rows, width), bf16)

    cost = pl.CostEstimate(
        flops=4 * rows * width * inner, bytes_accessed=4 * width * inner, transcendentals=0
    )

    def like(*arrays):
        return [jax.ShapeDtypeStruct(a.shape, a.dtype) for a in arrays]

    def forward(tick, incoming, weights, state):
        following, *state = pl.pallas_call(
            functools.partial(forward_kernel, tick, waves, sections),
            in_specs=[far, whole(), whole(), whole(), whole(), far, far, far],
            out_specs=[whole(), far, far, far],
            scratch_shapes=[
                pltpu.VMEM((rows, width), bf16),
                pltpu.VMEM((rows, width), bf16),
                pltpu.VMEM((rows, inner), f32),
                pltpu.VMEM((rows, inner), bf16),
                pltpu.VMEM((rows, features), bf16),
                pltpu.SemaphoreType.DMA((4,)),
            ],
            out_shape=[block, *like(*state)],
            input_output_aliases={5: 1, 6: 2, 7: 3},
            compiler_params=pltpu.CompilerParams(vmem_limit_bytes=14 * MEBI),
            cost_estimate=cost,
            name="forward_block",
        )(entries, incoming, norm_gain, weights, input_projection[0], *state)
        return following, state

    def backward(tick, incoming, weights, grads):
        return pl.pallas_call(
            functools.partial(backward_kernel, tick, waves, sections),
            in_specs=[far, whole(), far, far, far, whole(), whole(), whole(), far],
            out_specs=[whole(), far],
            scratch_shapes=[
                pltpu.VMEM((rows, width), bf16),
                pltpu.VMEM((rows, width), bf16),
                pltpu.VMEM((rows, inner), f32),
                pltpu.VMEM((rows, features), bf16),
                pltpu.VMEM((rows, width), f32),
                pltpu.VMEM((rows, inner), bf16),
                pltpu.VMEM((signals, features), f32),
                pltpu.SemaphoreType.DMA((5,)),
            ],
            out_shape=[block, *like(grads)],
            input_output_aliases={8: 1},
            compiler_params=pltpu.CompilerParams(vmem_limit_bytes=16 * MEBI),
            cost_estimate=cost,
            name="backward_block",
        )(targets, incoming, *state, norm_gain, weights, output_projection[0], grads)

    up = empty
    down = empty
    for tick in range(2 * sections + waves - 1):
        stages = [tick - m for m in range(waves)]
        back = [s for s in stages if sections <= s < 2 * sections]
        ahead = [s for s in stages if 0 <= s < sections]
        if back:
            down, grads = backward(tick, down, weights, grads)
            pairs = [(2 * sections - 1 - s, 2 * sections - 2 - s) for s in back if s < 2 * sections - 1]
            if pairs:
                down = lax.ppermute(down, "section", pairs)
        if ahead:
            up, state = forward(tick, up, weights, state)
            pairs = [(s, s + 1) for s in ahead if s < sections - 1]
            if pairs:
                up = lax.ppermute(up, "section", pairs)

    flat = grads.reshape(batches, SPLIT, signals * features).sum(axis=1) / length
    everyone = lax.all_to_all(
        jnp.broadcast_to(flat[None], (lax.axis_size("dp"), *flat.shape)), "dp", 0, 0, tiled=True
    ).reshape(-1, flat.shape[1])
    section_scores = pl.pallas_call(
        scores_kernel,
        out_shape=jax.ShapeDtypeStruct((batches, query_examples.shape[0]), f32),
        in_specs=[whole()] * 3,
        out_specs=whole(),
        compiler_params=pltpu.CompilerParams(vmem_limit_bytes=24 * MEBI),
        name="section_scores",
    )(query_examples[None], everyone, inverse)
    shares = lax.all_to_all(
        jnp.broadcast_to(section_scores[None], (sections, *section_scores.shape)),
        "section", 0, 0, tiled=True,
    )
    return shares.sum(axis=0)


def solution(mesh):
    placed = (
        P("dp", None),
        P("dp", None),
        P("dp"),
        P(),
        P("section", None),
        P("section", "dp", None),
        P("section", "dp", None),
        P("section", None, None),
        P("section", None, None),
        P("section", None, None),
    )
    return jax.shard_map(
        per_device, mesh=mesh, in_specs=placed, out_specs=P("dp", None), check_vma=False
    )
```

```python
import functools

import jax
import jax.numpy as jnp
from jax import lax
from jax.experimental import pallas as pl
from jax.experimental.pallas import tpu as pltpu
from jax.sharding import PartitionSpec as P

EXACT = lax.Precision.HIGHEST
BLOCK = 128
CHUNK = 512
HALF = 512
SPLIT = 2
f32 = jnp.float32
bf16 = jnp.bfloat16
NT = (((1,), (1,)), ((), ()))
TN = (((0,), (0,)), ((), ()))
MEBI = 1 << 20


def whole():
    return pl.BlockSpec(memory_space=pltpu.VMEM)


def swept(block):
    size = block.shape[0]
    lanes = lax.broadcasted_iota(jnp.int32, (1, size), 1)
    rows = lax.broadcasted_iota(jnp.int32, (size, 1), 0)
    for at in range(size):
        column = block[:, at : at + 1]
        row = block[at : at + 1, :]
        inverse = 1.0 / column[at : at + 1, :]
        scaled = jnp.where(lanes == at, -inverse, row * inverse)
        column = jnp.where(rows == at, -1.0, column)
        kept = jnp.where((lanes == at) | (rows == at), 0.0, block)
        block = kept - column * scaled
    return block


def exact_dot(a, b):
    return jnp.dot(a, b, precision=EXACT, preferred_element_type=f32)


def inverse_kernel(prior, out):
    size = prior.shape[0]
    tall = min(256, size)
    out[...] = prior[...]

    def step(turn, _):
        span = pl.ds(pl.multiple_of(turn * BLOCK, BLOCK), BLOCK)
        pivot = swept(out[span, span])
        left = out[:, span]
        above = out[span, :]
        right = -exact_dot(left, pivot)
        below = -exact_dot(pivot, above)
        for row in range(0, size, tall):
            out[row : row + tall, :] -= exact_dot(right[row : row + tall], above)
        out[:, span] = right
        out[span, :] = below
        out[span, span] = pivot
        return 0

    lax.fori_loop(0, size // BLOCK, step, 0)


def minus_inverse(prior):
    size = prior.shape[0]
    return pl.pallas_call(
        inverse_kernel,
        out_shape=jax.ShapeDtypeStruct(prior.shape, f32),
        in_specs=[whole()],
        out_specs=whole(),
        compiler_params=pltpu.CompilerParams(vmem_limit_bytes=32 * MEBI),
        cost_estimate=pl.CostEstimate(
            flops=60 * size**3, bytes_accessed=8 * size * size, transcendentals=0
        ),
        name="prior_inverse",
    )(prior)


def inverse_root(hidden):
    return lax.rsqrt(jnp.mean(hidden * hidden, axis=-1, keepdims=True) + 1e-05)


def moved(source, target, arrived, at):
    copy = pltpu.make_async_copy(source, target, arrived.at[at])
    copy.start()
    return copy


def nothing_kernel(*targets):
    pass


def load_kernel(source, target, arrived):
    moved(source, target, arrived, 0).wait()


def forward_kernel(
    tick, waves, sections, parity, entries, incoming, gain, weights, input_map, kept_hidden, kept_values,
    kept_features, following, hiddens, values_out, features_out,
    hidden, normed, values, activated, features, arrived,
):
    section = lax.axis_index("section")
    turn = tick - section
    width = incoming.shape[1]

    @pl.when((turn >= 0) & (turn < waves) & (section % 2 == parity))
    def _():
        @pl.when(section == 0)
        def _():
            moved(entries.at[turn], hidden, arrived, 0).wait()

        @pl.when(section != 0)
        def _():
            hidden[...] = incoming[...]

        saves = [moved(hidden, hiddens.at[turn], arrived, 1)]
        widened = hidden[...].astype(f32)
        normed[...] = (widened * inverse_root(widened) * gain[...].astype(f32)).astype(bf16)

        def inward(at, _):
            span = pl.ds(pl.multiple_of(at * HALF, HALF), HALF)
            part = jnp.dot(normed[...], weights[0, :, span], preferred_element_type=f32)
            values[:, span] = part
            activated[:, span] = (part * jax.nn.sigmoid(part)).astype(bf16)
            return 0

        lax.fori_loop(0, weights.shape[2] // HALF, inward, 0)
        saves.append(moved(values, values_out.at[turn], arrived, 2))

        @pl.when(section != sections - 1)
        def _():
            def outward(at, _):
                span = pl.ds(pl.multiple_of(at * CHUNK, CHUNK), CHUNK)
                branch = lax.dot_general(
                    activated[...], weights[1, span, :], NT, preferred_element_type=f32
                )
                following[:, span] = (hidden[:, span].astype(f32) + branch).astype(bf16)
                return 0

            lax.fori_loop(0, width // CHUNK, outward, 0)

        features[...] = lax.dot_general(
            normed[...], input_map[...], NT, preferred_element_type=f32
        ).astype(bf16)
        saves.append(moved(features, features_out.at[turn], arrived, 3))
        for copy in saves:
            copy.wait()


def backward_kernel(
    tick, waves, sections, parity, entries, incoming, hiddens, values_in, features_in, gain, weights,
    output_map, kept_grads, previous, grads_out,
    cotangent, hidden, values, features, weighted, slopes, grads, arrived,
):
    section = lax.axis_index("section")
    turn = tick - (2 * sections - 1 - section)
    rows, width = incoming.shape

    @pl.when((turn >= 0) & (turn < waves) & (section % 2 == parity))
    def _():
        values_here = moved(values_in.at[turn], values, arrived, 1)
        hidden_here = moved(hiddens.at[turn], hidden, arrived, 2)
        features_here = moved(features_in.at[turn], features, arrived, 3)

        @pl.when(section == sections - 1)
        def _():
            moved(entries.at[turn], cotangent, arrived, 0).wait()

        @pl.when(section != sections - 1)
        def _():
            cotangent[...] = incoming[...]

        values_here.wait()

        def inward(at, _):
            span = pl.ds(pl.multiple_of(at * HALF, HALF), HALF)
            upstream = jnp.dot(cotangent[...], weights[1, :, span], preferred_element_type=f32)
            here = values[:, span]
            logistic = jax.nn.sigmoid(here)
            slopes[:, span] = (upstream * logistic * (1.0 + here * (1.0 - logistic))).astype(bf16)
            return 0

        lax.fori_loop(0, weights.shape[2] // HALF, inward, 0)
        hidden_here.wait()
        features_here.wait()

        @pl.when(section != 0)
        def _():
            widened = hidden[...].astype(f32)
            factor = inverse_root(widened)

            def outward(at, inner):
                span = pl.ds(pl.multiple_of(at * CHUNK, CHUNK), CHUNK)
                part = lax.dot_general(
                    slopes[...], weights[0, span, :], NT, preferred_element_type=f32
                ) * gain[:, span].astype(f32)
                weighted[:, span] = part
                return inner + jnp.sum(
                    part * hidden[:, span].astype(f32), axis=-1, keepdims=True
                )

            inner = lax.fori_loop(0, width // CHUNK, outward, jnp.zeros((rows, 1), f32))
            pull = (factor * factor * factor) * (inner / width)
            hidden_grad = factor * weighted[...] - hidden[...].astype(f32) * pull
            previous[...] = (cotangent[...].astype(f32) + hidden_grad).astype(bf16)

        signals = lax.dot_general(
            slopes[...], output_map[...], NT, preferred_element_type=f32
        ).astype(bf16)
        grads[...] = lax.dot_general(signals, features[...], TN, preferred_element_type=f32)
        moved(grads, grads_out.at[turn], arrived, 4).wait()


def scores_kernel(queries, every, inverse, out):
    count = every.shape[0]
    batches, chosen = out.shape
    against = exact_dot(every[...], inverse[...])
    gram = -lax.dot_general(
        against, every[...], NT, precision=EXACT, preferred_element_type=f32
    )

    def counted(shape, axis):
        return lax.broadcasted_iota(jnp.int32, shape, axis)

    eye = (counted((count, count), 0) == counted((count, count), 1)).astype(f32)
    select = (counted((count, chosen), 0) == queries[...]).astype(f32)
    solved = -exact_dot(swept(gram + eye), exact_dot(gram, select))
    mine = lax.axis_index("dp") * batches + counted((batches, count), 0)
    own = (counted((batches, count), 1) == mine).astype(f32)
    out[...] = exact_dot(own, solved)


def per_device(
    inputs,
    output_cotangent,
    lengths,
    query_examples,
    norm_gain,
    value_weight,
    output_weight,
    input_projection,
    output_projection,
    fisher_prior,
):
    sections = lax.axis_size("section")
    batches = lengths.shape[0]
    length = inputs.shape[0] // batches
    waves = SPLIT * batches
    rows = length // SPLIT
    width = inputs.shape[1]
    inner = value_weight.shape[2]
    features = input_projection.shape[1]
    signals = output_projection.shape[1]
    both = jnp.concatenate([value_weight, output_weight], axis=0)
    weights = lax.all_gather(both, "dp", axis=1, tiled=True)
    entries = inputs.reshape(waves, rows, width)
    positions = jnp.arange(length, dtype=jnp.int32)
    keep = (positions[None, :] < lengths[:, None]).astype(bf16)
    targets = output_cotangent.reshape(batches, length, width) * keep[:, :, None]
    targets = targets.reshape(waves, rows, width)
    kinds = (
        ((waves, rows, width), bf16),
        ((waves, rows, inner), f32),
        ((waves, rows, features), bf16),
        ((waves, signals, features), f32),
        ((rows, width), bf16),
    )
    *state, grads, empty = pl.pallas_call(
        nothing_kernel,
        out_shape=[jax.ShapeDtypeStruct(*kind) for kind in kinds],
        out_specs=[whole()] * len(kinds),
        compiler_params=pltpu.CompilerParams(vmem_limit_bytes=8 * MEBI),
        name="room",
    )()
    weights, inverse, targets = lax.optimization_barrier(
        (weights, minus_inverse(fisher_prior[0]), targets)
    )
    far = pl.BlockSpec(memory_space=pltpu.HBM)
    weights = pltpu.with_memory_space_constraint(
        pl.pallas_call(
            load_kernel,
            out_shape=pltpu.VMEM(weights.shape, weights.dtype),
            in_specs=[far],
            out_specs=whole(),
            scratch_shapes=[pltpu.SemaphoreType.DMA((1,))],
            compiler_params=pltpu.CompilerParams(vmem_limit_bytes=40 * MEBI),
            name="weights_load",
        )(weights),
        pltpu.VMEM,
    )
    block = jax.ShapeDtypeStruct((rows, width), bf16)

    cost = pl.CostEstimate(
        flops=4 * rows * width * inner, bytes_accessed=4 * width * inner, transcendentals=0
    )

    def like(*arrays):
        return [jax.ShapeDtypeStruct(a.shape, a.dtype) for a in arrays]

    def forward(tick, parity, incoming, state):
        following, *state = pl.pallas_call(
            functools.partial(forward_kernel, tick, waves, sections, parity),
            in_specs=[far, whole(), whole(), whole(), whole(), far, far, far],
            out_specs=[whole(), far, far, far],
            scratch_shapes=[
                pltpu.VMEM((rows, width), bf16),
                pltpu.VMEM((rows, width), bf16),
                pltpu.VMEM((rows, inner), f32),
                pltpu.VMEM((rows, inner), bf16),
                pltpu.VMEM((rows, features), bf16),
                pltpu.SemaphoreType.DMA((4,)),
            ],
            out_shape=[block, *like(*state)],
            input_output_aliases={5: 1, 6: 2, 7: 3},
            compiler_params=pltpu.CompilerParams(vmem_limit_bytes=14 * MEBI),
            cost_estimate=cost,
            name="forward_block",
        )(entries, incoming, norm_gain, weights, input_projection[0], *state)
        return following, state

    def backward(tick, parity, incoming, grads):
        return pl.pallas_call(
            functools.partial(backward_kernel, tick, waves, sections, parity),
            in_specs=[far, whole(), far, far, far, whole(), whole(), whole(), far],
            out_specs=[whole(), far],
            scratch_shapes=[
                pltpu.VMEM((rows, width), bf16),
                pltpu.VMEM((rows, width), bf16),
                pltpu.VMEM((rows, inner), f32),
                pltpu.VMEM((rows, features), bf16),
                pltpu.VMEM((rows, width), f32),
                pltpu.VMEM((rows, inner), bf16),
                pltpu.VMEM((signals, features), f32),
                pltpu.SemaphoreType.DMA((5,)),
            ],
            out_shape=[block, *like(grads)],
            input_output_aliases={8: 1},
            compiler_params=pltpu.CompilerParams(vmem_limit_bytes=16 * MEBI),
            cost_estimate=cost,
            name="backward_block",
        )(targets, incoming, *state, norm_gain, weights, output_projection[0], grads)

    up = [empty, empty]
    down = [empty, empty]
    for tick in range(2 * sections + waves - 1):
        stages = [tick - m for m in range(waves)]
        back = [2 * sections - 1 - s for s in stages if sections <= s < 2 * sections]
        ahead = [s for s in stages if 0 <= s < sections]
        arriving = list(down)
        for parity in (0, 1):
            here = [s for s in back if s % 2 == parity]
            if here:
                previous, grads = backward(tick, parity, arriving[parity], grads)
                pairs = [(s, s - 1) for s in here if s > 0]
                if pairs:
                    down[1 - parity] = lax.ppermute(previous, "section", pairs)
        arriving = list(up)
        for parity in (1, 0):
            here = [s for s in ahead if s % 2 == parity]
            if here:
                following, state = forward(tick, parity, arriving[parity], state)
                pairs = [(s, s + 1) for s in here if s < sections - 1]
                if pairs:
                    up[1 - parity] = lax.ppermute(following, "section", pairs)

    flat = grads.reshape(batches, SPLIT, signals * features).sum(axis=1) / length
    everyone = lax.all_to_all(
        jnp.broadcast_to(flat[None], (lax.axis_size("dp"), *flat.shape)), "dp", 0, 0, tiled=True
    ).reshape(-1, flat.shape[1])
    section_scores = pl.pallas_call(
        scores_kernel,
        out_shape=jax.ShapeDtypeStruct((batches, query_examples.shape[0]), f32),
        in_specs=[whole()] * 3,
        out_specs=whole(),
        compiler_params=pltpu.CompilerParams(vmem_limit_bytes=24 * MEBI),
        name="section_scores",
    )(query_examples[None], everyone, inverse)
    shares = lax.all_to_all(
        jnp.broadcast_to(section_scores[None], (sections, *section_scores.shape)),
        "section", 0, 0, tiled=True,
    )
    return shares.sum(axis=0)


def solution(mesh):
    placed = (
        P("dp", None),
        P("dp", None),
        P("dp"),
        P(),
        P("section", None),
        P("section", "dp", None),
        P("section", "dp", None),
        P("section", None, None),
        P("section", None, None),
        P("section", None, None),
    )
    return jax.shard_map(
        per_device, mesh=mesh, in_specs=placed, out_specs=P("dp", None), check_vma=False
    )
```

```python
import functools

import jax
import jax.numpy as jnp
from jax import lax
from jax.experimental import pallas as pl
from jax.experimental.pallas import tpu as pltpu
from jax.sharding import PartitionSpec as P

EXACT = lax.Precision.HIGHEST
BLOCK = 128
CHUNK = 1024
SPLIT = 2
f32 = jnp.float32
bf16 = jnp.bfloat16
NT = (((1,), (1,)), ((), ()))
TN = (((0,), (0,)), ((), ()))
MEBI = 1 << 20


def whole():
    return pl.BlockSpec(memory_space=pltpu.VMEM)


def swept(block):
    size = block.shape[0]
    lanes = lax.broadcasted_iota(jnp.int32, (1, size), 1)
    rows = lax.broadcasted_iota(jnp.int32, (size, 1), 0)
    for at in range(size):
        column = block[:, at : at + 1]
        row = block[at : at + 1, :]
        inverse = 1.0 / column[at : at + 1, :]
        scaled = jnp.where(lanes == at, -inverse, row * inverse)
        column = jnp.where(rows == at, -1.0, column)
        kept = jnp.where((lanes == at) | (rows == at), 0.0, block)
        block = kept - column * scaled
    return block


def exact_dot(a, b):
    return jnp.dot(a, b, precision=EXACT, preferred_element_type=f32)


def inverse_kernel(prior, out):
    size = prior.shape[0]
    tall = min(256, size)
    out[...] = prior[...]

    def step(turn, _):
        span = pl.ds(pl.multiple_of(turn * BLOCK, BLOCK), BLOCK)
        pivot = swept(out[span, span])
        left = out[:, span]
        above = out[span, :]
        right = -exact_dot(left, pivot)
        below = -exact_dot(pivot, above)
        for row in range(0, size, tall):
            out[row : row + tall, :] -= exact_dot(right[row : row + tall], above)
        out[:, span] = right
        out[span, :] = below
        out[span, span] = pivot
        return 0

    lax.fori_loop(0, size // BLOCK, step, 0)


def minus_inverse(prior):
    size = prior.shape[0]
    return pl.pallas_call(
        inverse_kernel,
        out_shape=jax.ShapeDtypeStruct(prior.shape, f32),
        in_specs=[whole()],
        out_specs=whole(),
        compiler_params=pltpu.CompilerParams(vmem_limit_bytes=32 * MEBI),
        cost_estimate=pl.CostEstimate(
            flops=60 * size**3, bytes_accessed=8 * size * size, transcendentals=0
        ),
        name="prior_inverse",
    )(prior)


def inverse_root(hidden):
    return lax.rsqrt(jnp.mean(hidden * hidden, axis=-1, keepdims=True) + 1e-05)


def moved(source, target, arrived, at):
    copy = pltpu.make_async_copy(source, target, arrived.at[at])
    copy.start()
    return copy


def nothing_kernel(*targets):
    pass


def load_kernel(source, target, arrived):
    moved(source, target, arrived, 0).wait()


def forward_kernel(
    tick, low, high, waves, sections, entries, incoming, gain, weights, input_map, kept_hidden, kept_values,
    kept_features, following, hiddens, values_out, features_out,
    hidden, normed, values, activated, features, arrived,
):
    section = lax.axis_index("section")
    turn = tick - section
    width = incoming.shape[1]

    @pl.when((turn >= 0) & (turn < waves) & (section >= low) & (section < high))
    def _():
        @pl.when(section == 0)
        def _():
            moved(entries.at[turn], hidden, arrived, 0).wait()

        @pl.when(section != 0)
        def _():
            hidden[...] = incoming[...]

        saves = [moved(hidden, hiddens.at[turn], arrived, 1)]
        widened = hidden[...].astype(f32)
        normed[...] = (widened * inverse_root(widened) * gain[...].astype(f32)).astype(bf16)
        values[...] = jnp.dot(normed[...], weights[0], preferred_element_type=f32)
        saves.append(moved(values, values_out.at[turn], arrived, 2))
        activated[...] = (values[...] * jax.nn.sigmoid(values[...])).astype(bf16)

        @pl.when(section != sections - 1)
        def _():
            def outward(at, _):
                span = pl.ds(pl.multiple_of(at * CHUNK, CHUNK), CHUNK)
                branch = lax.dot_general(
                    activated[...], weights[1, span, :], NT, preferred_element_type=f32
                )
                following[:, span] = (hidden[:, span].astype(f32) + branch).astype(bf16)
                return 0

            lax.fori_loop(0, width // CHUNK, outward, 0)

        features[...] = lax.dot_general(
            normed[...], input_map[...], NT, preferred_element_type=f32
        ).astype(bf16)
        saves.append(moved(features, features_out.at[turn], arrived, 3))
        for copy in saves:
            copy.wait()


def backward_kernel(
    tick, waves, sections, entries, incoming, hiddens, values_in, features_in, gain, weights,
    output_map, kept_grads, previous, grads_out,
    cotangent, hidden, values, features, weighted, slopes, grads, arrived,
):
    section = lax.axis_index("section")
    turn = tick - (2 * sections - 1 - section)
    rows, width = incoming.shape

    @pl.when((turn >= 0) & (turn < waves))
    def _():
        values_here = moved(values_in.at[turn], values, arrived, 1)
        hidden_here = moved(hiddens.at[turn], hidden, arrived, 2)
        features_here = moved(features_in.at[turn], features, arrived, 3)

        @pl.when(section == sections - 1)
        def _():
            moved(entries.at[turn], cotangent, arrived, 0).wait()

        @pl.when(section != sections - 1)
        def _():
            cotangent[...] = incoming[...]

        upstream = jnp.dot(cotangent[...], weights[1], preferred_element_type=f32)
        values_here.wait()
        hidden_here.wait()
        features_here.wait()
        logistic = jax.nn.sigmoid(values[...])
        slopes[...] = (
            upstream * logistic * (1.0 + values[...] * (1.0 - logistic))
        ).astype(bf16)

        @pl.when(section != 0)
        def _():
            widened = hidden[...].astype(f32)
            factor = inverse_root(widened)

            def outward(at, inner):
                span = pl.ds(pl.multiple_of(at * CHUNK, CHUNK), CHUNK)
                part = lax.dot_general(
                    slopes[...], weights[0, span, :], NT, preferred_element_type=f32
                ) * gain[:, span].astype(f32)
                weighted[:, span] = part
                return inner + jnp.sum(
                    part * hidden[:, span].astype(f32), axis=-1, keepdims=True
                )

            inner = lax.fori_loop(0, width // CHUNK, outward, jnp.zeros((rows, 1), f32))
            pull = (factor * factor * factor) * (inner / width)
            hidden_grad = factor * weighted[...] - hidden[...].astype(f32) * pull
            previous[...] = (cotangent[...].astype(f32) + hidden_grad).astype(bf16)

        signals = lax.dot_general(
            slopes[...], output_map[...], NT, preferred_element_type=f32
        ).astype(bf16)
        grads[...] = lax.dot_general(signals, features[...], TN, preferred_element_type=f32)
        moved(grads, grads_out.at[turn], arrived, 4).wait()


def scores_kernel(queries, every, inverse, out):
    count = every.shape[0]
    batches, chosen = out.shape
    against = exact_dot(every[...], inverse[...])
    gram = -lax.dot_general(
        against, every[...], NT, precision=EXACT, preferred_element_type=f32
    )

    def counted(shape, axis):
        return lax.broadcasted_iota(jnp.int32, shape, axis)

    eye = (counted((count, count), 0) == counted((count, count), 1)).astype(f32)
    select = (counted((count, chosen), 0) == queries[...]).astype(f32)
    solved = -exact_dot(swept(gram + eye), exact_dot(gram, select))
    mine = lax.axis_index("dp") * batches + counted((batches, count), 0)
    own = (counted((batches, count), 1) == mine).astype(f32)
    out[...] = exact_dot(own, solved)


def per_device(
    inputs,
    output_cotangent,
    lengths,
    query_examples,
    norm_gain,
    value_weight,
    output_weight,
    input_projection,
    output_projection,
    fisher_prior,
):
    sections = lax.axis_size("section")
    batches = lengths.shape[0]
    length = inputs.shape[0] // batches
    waves = SPLIT * batches
    rows = length // SPLIT
    width = inputs.shape[1]
    inner = value_weight.shape[2]
    features = input_projection.shape[1]
    signals = output_projection.shape[1]
    both = jnp.concatenate([value_weight, output_weight], axis=0)
    weights = lax.all_gather(both, "dp", axis=1, tiled=True)
    entries = inputs.reshape(waves, rows, width)
    positions = jnp.arange(length, dtype=jnp.int32)
    keep = (positions[None, :] < lengths[:, None]).astype(bf16)
    targets = output_cotangent.reshape(batches, length, width) * keep[:, :, None]
    targets = targets.reshape(waves, rows, width)
    kinds = (
        ((waves, rows, width), bf16),
        ((waves, rows, inner), f32),
        ((waves, rows, features), bf16),
        ((waves, signals, features), f32),
        ((rows, width), bf16),
    )
    *state, grads, empty = pl.pallas_call(
        nothing_kernel,
        out_shape=[jax.ShapeDtypeStruct(*kind) for kind in kinds],
        out_specs=[whole()] * len(kinds),
        compiler_params=pltpu.CompilerParams(vmem_limit_bytes=8 * MEBI),
        name="room",
    )()
    weights, inverse, targets = lax.optimization_barrier(
        (weights, minus_inverse(fisher_prior[0]), targets)
    )
    far = pl.BlockSpec(memory_space=pltpu.HBM)
    weights = pltpu.with_memory_space_constraint(
        pl.pallas_call(
            load_kernel,
            out_shape=pltpu.VMEM(weights.shape, weights.dtype),
            in_specs=[far],
            out_specs=whole(),
            scratch_shapes=[pltpu.SemaphoreType.DMA((1,))],
            compiler_params=pltpu.CompilerParams(vmem_limit_bytes=40 * MEBI),
            name="weights_load",
        )(weights),
        pltpu.VMEM,
    )
    block = jax.ShapeDtypeStruct((rows, width), bf16)

    cost = pl.CostEstimate(
        flops=4 * rows * width * inner, bytes_accessed=4 * width * inner, transcendentals=0
    )

    def like(*arrays):
        return [jax.ShapeDtypeStruct(a.shape, a.dtype) for a in arrays]

    def forward(tick, low, high, incoming, state):
        following, *state = pl.pallas_call(
            functools.partial(forward_kernel, tick, low, high, waves, sections),
            in_specs=[far, whole(), whole(), whole(), whole(), far, far, far],
            out_specs=[whole(), far, far, far],
            scratch_shapes=[
                pltpu.VMEM((rows, width), bf16),
                pltpu.VMEM((rows, width), bf16),
                pltpu.VMEM((rows, inner), f32),
                pltpu.VMEM((rows, inner), bf16),
                pltpu.VMEM((rows, features), bf16),
                pltpu.SemaphoreType.DMA((4,)),
            ],
            out_shape=[block, *like(*state)],
            input_output_aliases={5: 1, 6: 2, 7: 3},
            compiler_params=pltpu.CompilerParams(vmem_limit_bytes=14 * MEBI),
            cost_estimate=cost,
            name="forward_block",
        )(entries, incoming, norm_gain, weights, input_projection[0], *state)
        return following, state

    def backward(tick, incoming, grads):
        return pl.pallas_call(
            functools.partial(backward_kernel, tick, waves, sections),
            in_specs=[far, whole(), far, far, far, whole(), whole(), whole(), far],
            out_specs=[whole(), far],
            scratch_shapes=[
                pltpu.VMEM((rows, width), bf16),
                pltpu.VMEM((rows, width), bf16),
                pltpu.VMEM((rows, inner), f32),
                pltpu.VMEM((rows, features), bf16),
                pltpu.VMEM((rows, width), f32),
                pltpu.VMEM((rows, inner), bf16),
                pltpu.VMEM((signals, features), f32),
                pltpu.SemaphoreType.DMA((5,)),
            ],
            out_shape=[block, *like(grads)],
            input_output_aliases={8: 1},
            compiler_params=pltpu.CompilerParams(vmem_limit_bytes=16 * MEBI),
            cost_estimate=cost,
            name="backward_block",
        )(targets, incoming, *state, norm_gain, weights, output_projection[0], grads)

    up = empty
    down = empty
    final = sections - 1

    def ahead_of(tick, high):
        return [tick - m for m in range(waves) if 0 <= tick - m < high]

    for tick in range(2 * sections + waves - 1):
        back = [2 * sections - 1 - tick + m for m in range(waves)]
        back = [s for s in back if 0 <= s < sections]
        if back:
            down, grads = backward(tick, down, grads)
            pairs = [(s, s - 1) for s in back if s > 0]
            if pairs:
                down = lax.ppermute(down, "section", pairs)
        if tick < sections:
            up, state = forward(tick, 0, sections, up, state)
            pairs = [(s, s + 1) for s in ahead_of(tick, final)]
            up = lax.ppermute(up, "section", pairs)
            continue
        late = ahead_of(tick - 1, final)
        if tick > sections and late:
            following, state = forward(tick - 1, 0, final, up, state)
            up = lax.ppermute(following, "section", [(s, s + 1) for s in late])
        if tick - final < waves:
            _, state = forward(tick, final, sections, up, state)

    flat = grads.reshape(batches, SPLIT, signals * features).sum(axis=1) / length
    everyone = lax.all_to_all(
        jnp.broadcast_to(flat[None], (lax.axis_size("dp"), *flat.shape)), "dp", 0, 0, tiled=True
    ).reshape(-1, flat.shape[1])
    section_scores = pl.pallas_call(
        scores_kernel,
        out_shape=jax.ShapeDtypeStruct((batches, query_examples.shape[0]), f32),
        in_specs=[whole()] * 3,
        out_specs=whole(),
        compiler_params=pltpu.CompilerParams(vmem_limit_bytes=24 * MEBI),
        name="section_scores",
    )(query_examples[None], everyone, inverse)
    shares = lax.all_to_all(
        jnp.broadcast_to(section_scores[None], (sections, *section_scores.shape)),
        "section", 0, 0, tiled=True,
    )
    return shares.sum(axis=0)


def solution(mesh):
    placed = (
        P("dp", None),
        P("dp", None),
        P("dp"),
        P(),
        P("section", None),
        P("section", "dp", None),
        P("section", "dp", None),
        P("section", None, None),
        P("section", None, None),
        P("section", None, None),
    )
    return jax.shard_map(
        per_device, mesh=mesh, in_specs=placed, out_specs=P("dp", None), check_vma=False
    )
```
